512 devices in a mesh: wide: 64 (over y, x, core), narrow: 8 (over z).
Axes of the slice: x: 4, y: 8, z: 8, core: 2. Of those that a mesh axis runs over, the one named last changes fastest.
Arguments:
- activations: bfloat16 [2048, 8192], P('wide', 'narrow'), may hold values from -6 to 6
- up_weight: bfloat16 [8192, 28672], P('narrow', 'wide'), may hold values from -0.0625 to 0.0625
- shrink_pool: bfloat16 [64, 8192, 64], P('wide', 'narrow'), may hold values from -0.0625 to 0.0625
- expand_pool: bfloat16 [64, 64, 28672], P('wide'), may hold values from -0.375 to 0.375
- row_adapter: int32 [2048, 1], replicated, may hold values from 0 to 63; in each aligned block of 256 rows (0 to 255, 256 to 511, ...) at most 16 rows name the same one
- holder_slot: int32 [64], replicated, may hold values from 0 to 63, each once
Outputs:
- projected: bfloat16 [2048, 28672], P('narrow', 'wide')
The draws below stay inside these ranges and needn't reach their ends.
Inputs may be any that keep to these rules, and one draw needn't show every extreme that they name: `row_adapter`: every adapter id is used by at least one row; popularity is uneven. In each aligned block of 256 rows, the rows of one row group, no adapter id is used by more than 16 rows. `holder_slot`: each pool position appears exactly once.
All inputs are finite; a program needn't handle non-finite values.
Results may differ from the reference program's by a relative error of at most 0.004.
Values may be sent and summed in bfloat16 or wider, within the bound.
No kernel may reach another device: no remote copies, remote signals or barrier semaphores. Data moves between devices by JAX's collectives and lax.ppermute only.
A program may use at most 64 MiB of HBM per device.

```python
import math
import jax
import jax.numpy as jnp
import numpy as np
from jax import lax

D = 8192
FF = 28672
R = 64
CAP = 16
ROWS = 2048
POOL = 64
N_NARROW = 8


def steps_of(key, shape, cuts, smallest, largest):
    def one(axis_at, parts):
        heights = jax.random.uniform(jax.random.fold_in(jax.random.fold_in(key, 6), axis_at), (parts,), jnp.float32, smallest / len(cuts), largest / len(cuts))
        return jnp.repeat(jnp.exp(heights), shape[axis_at] // parts).reshape((-1,) + (1,) * (len(shape) - axis_at - 1))

    factor_of = one(*cuts[0])
    for cut in cuts[1:]:
        factor_of = factor_of * one(*cut)
    return factor_of


def shared_out(key, own, number, rows, amount, top, bound, lean):
    sequence = jax.random.permutation(key, amount)
    heavy_load, ordinary = load_shares(amount, rows * top, bound, lean, True), load_shares(amount, rows * top, bound, lean, False)
    places = jnp.arange(amount)

    def named(tallies, offset_by):
        used = int((tallies > 0).sum())
        fixed = max(1, used // 4)
        moved = fixed + (places - fixed + offset_by * (used - fixed)) % max(1, amount - fixed)
        return jnp.zeros((amount,), jnp.int32).at[sequence[jnp.where(places < fixed, places, moved)]].set(jnp.asarray(tallies, jnp.int32))

    tallies = jnp.where(number % 4 == 0, named(heavy_load, number // 4), named(ordinary, number - number // 4 - 1))
    mixed = jax.random.permutation(jax.random.fold_in(own, 3), amount)
    donor, taker = mixed[0:amount // 2 * 2:2], mixed[1:amount // 2 * 2:2]
    slack = jnp.minimum(tallies[donor] - 1, bound - tallies[taker]) // 2
    slack = jnp.where((donor == sequence[0]) | (taker == sequence[0]) | (tallies[taker] == 0), 0, jnp.maximum(slack, 0))
    moved = jax.random.randint(jax.random.fold_in(own, 4), (amount // 2,), 0, 1 << 20) % (slack + 1)
    tallies = tallies.at[donor].add(-moved).at[taker].add(moved)
    items = jnp.searchsorted(jnp.cumsum(tallies), jnp.arange(rows * top), side="right").astype(jnp.int32)
    grid = items.reshape(top, rows).T
    grid = grid[jax.random.permutation(jax.random.fold_in(own, 1), rows)]
    offset_by = jax.random.randint(jax.random.fold_in(own, 2), (rows, 1), 0, top)
    return jnp.take_along_axis(grid, (jnp.arange(top)[None, :] + offset_by) % top, axis=1)


def load_shares(count, total, most, skew, full):
    loads = [(1 << 20) // math.isqrt(grade ** skew) + 1 for grade in range(1, count + 1)]
    largest = most if full else min(most, max(-(-total // count), total * loads[0] // sum(loads)))
    least = 1 if total - largest >= count - 1 else 0
    holding, surplus = [largest] + [least] * (count - 1), total - largest - least * (count - 1)
    while surplus > 0:
        free = [i for i in range(1, count) if holding[i] < largest] or [i for i in range(1, count) if holding[i] < most]
        mass, left = sum([loads[i] for i in free]), surplus
        for i in free:
            extra = min(most - holding[i], max(1, left * loads[i] // mass), surplus)
            holding[i] = holding[i] + extra
            surplus = surplus - extra
    return np.array(holding)


def centred(rng, shape, scale, reach, split=(), kind=jnp.bfloat16):
    entries = scale * jax.random.normal(rng, shape, jnp.float32)
    if split:
        entries = entries * steps_of(rng, shape, split, -0.22, 0.18)
    return jnp.clip(entries, -reach, reach).astype(kind)


def setup_inputs(seed: int = 0) -> dict:
    key_of = jax.random.split(jax.random.key(seed), 7)
    activations = centred(key_of[0], (ROWS, D), 1.0, 6.0, ((0, 64), (1, 8)))
    up_weight = centred(key_of[1], (D, FF), D ** -0.5, 0.0625, ((0, 8), (1, 64)))
    shrink_pool = centred(key_of[2], (POOL, D, R), D ** -0.5, 0.0625, ((0, 64), (1, 8)))
    expand_pool = centred(key_of[3], (POOL, R, FF), (4 * R) ** -0.5, 0.375, ((0, 64),))
    row_adapter_keys = jax.random.split(jax.random.fold_in(key_of[4], 1), ROWS // (ROWS // N_NARROW))
    row_adapter_turns = jax.random.permutation(jax.random.fold_in(key_of[4], 3), ROWS // (ROWS // N_NARROW))
    row_adapter = jax.vmap(lambda own, number: shared_out(jax.random.fold_in(key_of[4], 2), own, number, ROWS // N_NARROW, POOL, 1, CAP, 2))(row_adapter_keys, row_adapter_turns).reshape((ROWS, 1))
    holder_slot = jax.random.permutation(key_of[5], POOL).astype(jnp.int32)
    return {"activations": activations, "up_weight": up_weight, "shrink_pool": shrink_pool, "expand_pool": expand_pool, "row_adapter": row_adapter, "holder_slot": holder_slot}


def reference(activations, up_weight, shrink_pool, expand_pool, row_adapter, holder_slot):
    base = jnp.dot(activations, up_weight, preferred_element_type=jnp.float32)
    position = holder_slot[row_adapter[:, 0]].astype(jnp.int32)

    def down_projection_row(item):
        single, slot = item
        return jnp.dot(single[None, :], shrink_pool[slot], preferred_element_type=jnp.float32)[0]

    shrunk = lax.map(down_projection_row, (activations, position)).astype(jnp.bfloat16)

    def expand_row(item):
        reduced_rank_output, slot = item
        return jnp.dot(reduced_rank_output[None, :], expand_pool[slot], preferred_element_type=jnp.float32)[0]

    adapter_update = lax.map(expand_row, (shrunk, position))
    return (base + 2.0 * adapter_update).astype(jnp.bfloat16)
```

```python
import jax
import jax.numpy as jnp
from jax import lax
from jax.sharding import Mesh
from jax.sharding import PartitionSpec as P

CAP = 16
ADAPTER_SCALE = 2.0
Y, X, C, Z = "wide_y", "wide_x", "wide_c", "narrow"
WIDE = (Y, X, C)
BF16, F32 = jnp.bfloat16, jnp.float32
HIGHEST = lax.Precision.HIGHEST


def shifted(value, axis, step):
    size = lax.axis_size(axis)
    return lax.ppermute(value, axis, [(i, (i + step) % size) for i in range(size)])


def from_everyone(shard, axis):
    devices = lax.axis_size(axis)
    return lax.all_to_all(
        jnp.broadcast_to(shard[None], (devices, *shard.shape)), axis, 0, 0, tiled=True
    )


def sum_at_owner(parts):
    size = lax.axis_size(Z)
    me = lax.axis_index(Z)

    def own(offset):
        return lax.dynamic_index_in_dim(parts, (me + offset) % size, 0, keepdims=False)

    far = size // 2
    up = own(far)
    for offset in range(far - 1, -1, -1):
        up = shifted(up.astype(BF16), Z, 1).astype(F32)
        if offset:
            up = up + own(offset)
    down = own(far + 1)
    for offset in range(far + 2, size + 1):
        down = shifted(down.astype(BF16), Z, -1).astype(F32)
        if offset < size:
            down = down + own(offset)
    return own(0) + up + down


def per_device(activations, up_weight, shrink_pool, expand_pool, row_adapter, holder_slot):
    n_y, n_x, n_c, n_z = (lax.axis_size(a) for a in (Y, X, C, Z))
    block_rows = activations.shape[0]
    columns = up_weight.shape[1]
    rank = shrink_pool.shape[2]
    pool = holder_slot.shape[0]
    me_c, me_z = lax.axis_index(C), lax.axis_index(Z)
    chip = lax.axis_index(Y) * n_x + lax.axis_index(X)

    own_weight, own_shrink = up_weight.T, shrink_pool[0].T
    mine = jnp.concatenate([own_weight, own_shrink], axis=0)
    other = shifted(mine, C, 1)
    weights = jnp.concatenate([own_weight, other[:columns]], axis=0)
    other_shrink = other[columns:]
    shrinks = jnp.where(
        me_c == 0,
        jnp.concatenate([own_shrink, other_shrink], axis=0),
        jnp.concatenate([other_shrink, own_shrink], axis=0),
    )

    position = jnp.sum(
        jnp.where(
            row_adapter[:, 0][:, None] == jnp.arange(pool, dtype=jnp.int32)[None, :],
            holder_slot[None, :],
            0,
        ),
        axis=1,
    )
    grouped = position.reshape(n_z, -1)
    group_rows = grouped.shape[1]
    earlier = (
        jnp.arange(group_rows, dtype=jnp.int32)[:, None]
        > jnp.arange(group_rows, dtype=jnp.int32)[None, :]
    )
    place = jnp.sum(
        jnp.where(earlier[None] & (grouped[:, :, None] == grouped[:, None, :]), 1, 0), axis=2
    ).astype(jnp.int32)

    along_y = from_everyone(activations, Y)
    along_x = from_everyone(along_y, X)
    rows = jnp.transpose(along_x, (1, 0, 2, 3)).reshape(n_y, n_x * block_rows, -1)

    low = jnp.einsum("nk,yrk->ynr", shrinks, rows, preferred_element_type=F32)
    low = low.reshape(n_y, n_c, rank, n_x * block_rows)

    def of_core(table):
        parted = table.reshape(n_z, n_x, n_c, block_rows)
        return lax.dynamic_index_in_dim(parted, me_c, 2, keepdims=False).reshape(n_z, -1)

    core_position, core_place = of_core(grouped), of_core(place)
    adapters_here = chip * n_c + jnp.arange(n_c, dtype=jnp.int32)
    picked = (core_position[:, None, None, :] == adapters_here[None, :, None, None]) & (
        core_place[:, None, None, :] == jnp.arange(CAP, dtype=jnp.int32)[None, None, :, None]
    )
    packed = jnp.einsum(
        "yasr,yanr->aysn", picked.astype(F32), low, precision=HIGHEST, preferred_element_type=F32
    )
    packed = packed.reshape(n_c * n_z, CAP // 2, 2 * rank)
    gathered = lax.all_to_all(packed, (C, Z), 0, 0, tiled=True)
    shrunk = jnp.sum(gathered, axis=0).reshape(CAP, rank).astype(BF16)

    pieces = jnp.dot(shrunk, expand_pool[0], preferred_element_type=F32).astype(BF16)
    pieces = jnp.transpose(pieces.reshape(CAP, pool, columns), (1, 0, 2))
    received = lax.all_to_all(pieces, WIDE, 0, 0, tiled=True).reshape(pool * CAP, columns)

    partial = jnp.einsum("nk,yrk->ynr", weights, rows, preferred_element_type=F32)
    base = sum_at_owner(partial)
    base_here, base_there = base[:columns], base[columns:]
    base_from = shifted(base_there, C, 1)

    group_position = lax.dynamic_index_in_dim(grouped, me_z, 0, keepdims=False)
    group_place = lax.dynamic_index_in_dim(place, me_z, 0, keepdims=False)
    slot_of_row = group_position * CAP + group_place
    chosen = (
        jnp.arange(pool * CAP, dtype=jnp.int32)[:, None] == slot_of_row[None, :]
    ).astype(BF16)
    update = lax.dot_general(
        received, chosen, (((0,), (0,)), ((), ())), preferred_element_type=F32
    )
    row = jnp.arange(group_rows, dtype=jnp.int32)
    row_core = (row // block_rows) % n_c
    row_in_core = (row // (block_rows * n_c)) * block_rows + row % block_rows
    source = jnp.where(row_core == me_c, 0, n_x * block_rows) + row_in_core
    spread = (jnp.arange(group_rows, dtype=jnp.int32)[:, None] == source[None, :]).astype(F32)
    base_rows = jnp.dot(
        jnp.concatenate([base_here, base_from], axis=1),
        spread,
        precision=HIGHEST,
        preferred_element_type=F32,
    )
    return (base_rows + ADAPTER_SCALE * update).astype(BF16).T


def solution(mesh):
    finer = Mesh(mesh.devices.reshape(8, 4, 2, mesh.shape["narrow"]), (Y, X, C, Z))
    return jax.shard_map(
        per_device,
        mesh=finer,
        in_specs=(
            P(WIDE, Z),
            P(Z, WIDE),
            P(WIDE, Z, None),
            P(WIDE, None, None),
            P(),
            P(),
        ),
        out_specs=P(Z, WIDE),
        check_vma=False,
    )
```

```python
import functools

import jax
import jax.numpy as jnp
from jax import lax
from jax.sharding import Mesh
from jax.sharding import PartitionSpec as P

from jax.experimental import pallas as pl
from jax.experimental.pallas import tpu as pltpu


CAP = 16
ADAPTER_SCALE = 2.0
Y, X, C, ZH, ZL = "wide_y", "wide_x", "wide_c", "narrow_h", "narrow_l"
WIDE = (Y, X, C)
Z = (ZH, ZL)
BF16, F32 = jnp.bfloat16, jnp.float32
HIGHEST = lax.Precision.HIGHEST


def shifted(value, axis, step):
    size = lax.axis_size(axis)
    return lax.ppermute(value, axis, [(i, (i + step) % size) for i in range(size)])


def from_everyone(shard, axis):
    devices = lax.axis_size(axis)
    return lax.all_to_all(
        jnp.broadcast_to(shard[None], (devices, *shard.shape)), axis, 0, 0, tiled=True
    )


def sum_at_owner(parts):
    size = lax.axis_size(ZH)
    me = lax.axis_index(ZH)

    def own(offset):
        return lax.dynamic_index_in_dim(parts, (me + offset) % size, 0, keepdims=False)

    total = own(0)
    terms = [shifted(own(step).astype(BF16), ZH, step) for step in range(1, size)]
    for term in terms:
        total = total + term.astype(F32)
    return total


def expand_kernel(columns, terms_ref, factor_ref, out_ref, shrunk_ref):
    @pl.when(pl.program_id(0) == 0)
    def _():
        total = jnp.sum(terms_ref[...], axis=0)
        rank = total.shape[1] // 2
        half = total.shape[0]
        shrunk_ref[:half] = total[:, :rank]
        shrunk_ref[half:] = total[:, rank:]

    piece = jnp.dot(
        shrunk_ref[...].astype(BF16), factor_ref[...], preferred_element_type=F32
    )
    for i in range(out_ref.shape[0]):
        out_ref[i] = piece[:, i * columns : (i + 1) * columns].astype(BF16)


def expanded(terms, factor, pool, columns):
    together = 16
    rank, width = factor.shape
    return pl.pallas_call(
        functools.partial(expand_kernel, columns),
        grid=(pool // together,),
        in_specs=[
            pl.BlockSpec(terms.shape, lambda i: (0, 0, 0)),
            pl.BlockSpec((rank, together * columns), lambda i: (0, i)),
        ],
        out_specs=pl.BlockSpec((together, CAP, columns), lambda i: (i, 0, 0)),
        out_shape=jax.ShapeDtypeStruct((pool, CAP, columns), BF16),
        scratch_shapes=[pltpu.VMEM((CAP, rank), F32)],
        cost_estimate=pl.CostEstimate(
            flops=2 * CAP * rank * width, bytes_accessed=2 * (rank + CAP) * width, transcendentals=0
        ),
    )(terms, factor)


def per_device(activations, up_weight, shrink_pool, expand_pool, row_adapter, holder_slot):
    block_rows = activations.shape[0]
    columns = up_weight.shape[1]
    rank = shrink_pool.shape[2]
    pool = holder_slot.shape[0]
    n_z, n_x, n_c = lax.axis_size(Z), lax.axis_size(X), lax.axis_size(C)
    me_y, me_x, me_c, me_z = (lax.axis_index(a) for a in (Y, X, C, Z))
    me_zl = lax.axis_index(ZL)

    line_rows = from_everyone(activations, Y)

    own_shrink = shrink_pool[0].T
    near = jnp.concatenate(
        [own_shrink] + [shifted(own_shrink, X, step) for step in range(1, n_x)], axis=0
    )
    far = shifted(near, C, 1)

    own_weight = up_weight.T
    plane_weight = shifted(own_weight, ZL, 1)
    core_own = shifted(own_weight, C, 1)
    core_weights = core_own, shifted(plane_weight, C, 1)

    position = jnp.sum(
        jnp.where(
            row_adapter[:, 0][:, None] == jnp.arange(pool, dtype=jnp.int32)[None, :],
            holder_slot[None, :],
            0,
        ),
        axis=1,
    )
    grouped = position.reshape(n_z, -1)
    group_rows = grouped.shape[1]
    earlier = (
        jnp.arange(group_rows, dtype=jnp.int32)[:, None]
        > jnp.arange(group_rows, dtype=jnp.int32)[None, :]
    )
    place = jnp.sum(
        jnp.where(earlier[None] & (grouped[:, :, None] == grouped[:, None, :]), 1, 0), axis=2
    ).astype(jnp.int32)

    paired = line_rows.reshape(n_z // 2, 2, block_rows, -1)
    kept = lax.dynamic_index_in_dim(paired, me_zl, 1, keepdims=False)
    given = lax.dynamic_index_in_dim(paired, 1 - me_zl, 1, keepdims=False)
    taken = shifted(given, ZL, 1)
    blocks = jnp.stack([kept, taken])
    across = [blocks] + [shifted(blocks, X, step) for step in range(1, n_x)]

    def of_line(table):
        blocks = table.reshape(n_z, n_x * n_c, block_rows)
        return lax.dynamic_index_in_dim(blocks, me_x * n_c + me_c, 1, keepdims=False).reshape(-1)

    line_position, line_place = of_line(grouped), of_line(place)
    held_x = (me_x - jnp.arange(n_x, dtype=jnp.int32)) % n_x
    low = []
    for factors, core in ((near, me_c), (far, 1 - me_c)):
        held = (me_y * n_x + held_x) * n_c + core
        product = jnp.einsum("gik,nk->gin", line_rows, factors, preferred_element_type=F32)
        product = product.reshape(n_z * block_rows, n_x, rank)
        low.append(
            jnp.sum(
                jnp.where((line_position[:, None] == held[None])[..., None], product, 0.0), axis=1
            )
        )
    low = low[0] + low[1]
    line_group = jnp.arange(n_z * block_rows, dtype=jnp.int32) // block_rows
    local = line_position - me_y * (n_x * n_c)
    slots = n_x * n_c * n_z * CAP
    slot = jnp.where(
        (local >= 0) & (local < n_x * n_c), (local * n_z + line_group) * CAP + line_place, -1
    )
    half = CAP // 2
    slot_half = (slot // half) % 2
    slot_line = jnp.where(slot >= 0, (slot // CAP) * half + slot % half, -1)
    lines = jnp.arange(slots // 2, dtype=jnp.int32)[:, None]
    placed = jnp.concatenate(
        [
            ((lines == slot_line[None, :]) & (slot_half[None, :] == side)).astype(F32)
            for side in range(2)
        ],
        axis=1,
    )
    none = jnp.zeros_like(low)
    sides = jnp.concatenate(
        [jnp.concatenate([low, none], axis=1), jnp.concatenate([none, low], axis=1)], axis=0
    )
    packed = jnp.dot(placed, sides, precision=HIGHEST, preferred_element_type=F32)
    packed = packed.reshape(n_x * n_c * n_z, half, 2 * rank)
    gathered = lax.all_to_all(packed, (X, C, ZH, ZL), 0, 0, tiled=True)

    pieces = expanded(gathered, expand_pool[0], pool, columns)
    received = lax.all_to_all(pieces, WIDE, 0, 0, tiled=True)
    received = received.reshape(pool * CAP, columns)

    weights = [
        jnp.concatenate([own_weight, core_weights[0]], axis=0),
        jnp.concatenate([plane_weight, core_weights[1]], axis=0),
    ]
    rows = jnp.concatenate(across, axis=2)
    partial = sum(
        jnp.einsum("grk,nk->grn", rows[i], weights[i], preferred_element_type=F32)
        for i in range(2)
    )
    base = sum_at_owner(partial)
    mine = jnp.concatenate([base[:, :columns], shifted(base[:, columns:], C, 1)], axis=0)

    group_position = lax.dynamic_index_in_dim(grouped, me_z, 0, keepdims=False)
    group_place = lax.dynamic_index_in_dim(place, me_z, 0, keepdims=False)
    slot_of_row = group_position * CAP + group_place
    chosen = (
        jnp.arange(pool * CAP, dtype=jnp.int32)[:, None] == slot_of_row[None, :]
    ).astype(BF16)
    update = lax.dot_general(
        received, chosen, (((0,), (0,)), ((), ())), preferred_element_type=F32
    )
    row = jnp.arange(group_rows, dtype=jnp.int32)
    block = row // block_rows
    row_x, row_c = block // n_c, block % n_c
    source = (
        (row_c ^ me_c) * n_x + (me_x - row_x) % n_x
    ) * block_rows + row % block_rows
    spread = (jnp.arange(group_rows, dtype=jnp.int32)[:, None] == source[None, :]).astype(F32)
    base_rows = lax.dot_general(
        mine, spread, (((0,), (0,)), ((), ())), precision=HIGHEST, preferred_element_type=F32
    )
    return (base_rows + ADAPTER_SCALE * update).astype(BF16).T


def solution(mesh):
    finer = Mesh(mesh.devices.reshape(8, 4, 2, 4, 2), (Y, X, C, ZH, ZL))

    return jax.shard_map(
        per_device,
        mesh=finer,
        in_specs=(
            P(WIDE, Z),
            P(Z, WIDE),
            P(WIDE, Z, None),
            P(WIDE, None, None),
            P(),
            P(),
        ),
        out_specs=P(Z, WIDE),
        check_vma=False,
    )
```

```python
import functools

import jax
import jax.numpy as jnp
from jax import lax
from jax.sharding import Mesh
from jax.sharding import PartitionSpec as P

from jax.experimental import pallas as pl
from jax.experimental.pallas import tpu as pltpu


CAP = 16
ADAPTER_SCALE = 2.0
Y, X, C, ZH, ZL = "wide_y", "wide_x", "wide_c", "narrow_h", "narrow_l"
WIDE = (Y, X, C)
Z = (ZH, ZL)
BF16, F32 = jnp.bfloat16, jnp.float32
HIGHEST = lax.Precision.HIGHEST


def shifted(value, axis, step):
    size = lax.axis_size(axis)
    return lax.ppermute(value, axis, [(i, (i + step) % size) for i in range(size)])


def from_everyone(shard, axis):
    devices = lax.axis_size(axis)
    return lax.all_to_all(
        jnp.broadcast_to(shard[None], (devices, *shard.shape)), axis, 0, 0, tiled=True
    )


def sum_at_owner(parts):
    size = lax.axis_size(ZH)
    me = lax.axis_index(ZH)

    def own(offset):
        return lax.dynamic_index_in_dim(parts, (me + offset) % size, 0, keepdims=False)

    total = own(0)
    terms = [shifted(own(step).astype(BF16), ZH, step) for step in range(1, size)]
    for term in terms:
        total = total + term.astype(F32)
    return total


def expand_kernel(columns, terms_ref, factor_ref, out_ref):
    total = jnp.sum(terms_ref[...], axis=0)
    rank = total.shape[1] // 2
    shrunk = jnp.concatenate([total[:, :rank], total[:, rank:]], axis=0).astype(BF16)
    together = 8
    for first in range(0, out_ref.shape[0], together):
        piece = jnp.dot(
            shrunk,
            factor_ref[:, first * columns : (first + together) * columns],
            preferred_element_type=F32,
        )
        for i in range(together):
            out_ref[first + i] = piece[:, i * columns : (i + 1) * columns].astype(BF16)


def expanded(terms, factor, pool, columns):
    rank, width = factor.shape
    return pl.pallas_call(
        functools.partial(expand_kernel, columns),
        in_specs=[pl.BlockSpec(memory_space=pltpu.VMEM)] * 2,
        out_specs=pl.BlockSpec(memory_space=pltpu.VMEM),
        out_shape=jax.ShapeDtypeStruct((pool, CAP, columns), BF16),
        cost_estimate=pl.CostEstimate(
            flops=2 * CAP * rank * width, bytes_accessed=2 * (rank + CAP) * width, transcendentals=0
        ),
        compiler_params=pltpu.CompilerParams(vmem_limit_bytes=24 << 20),
    )(terms, factor)


def per_device(activations, up_weight, shrink_pool, expand_pool, row_adapter, holder_slot):
    block_rows = activations.shape[0]
    columns = up_weight.shape[1]
    rank = shrink_pool.shape[2]
    pool = holder_slot.shape[0]
    n_z, n_x, n_c = lax.axis_size(Z), lax.axis_size(X), lax.axis_size(C)
    me_y, me_x, me_c, me_z = (lax.axis_index(a) for a in (Y, X, C, Z))
    me_zl = lax.axis_index(ZL)

    line_rows = from_everyone(activations, Y)

    own_shrink = shrink_pool[0].T
    near = jnp.concatenate(
        [own_shrink] + [shifted(own_shrink, X, step) for step in range(1, n_x)], axis=0
    )
    far = shifted(near, C, 1)

    own_weight = up_weight.T
    plane_weight = shifted(own_weight, ZL, 1)
    core_own = shifted(own_weight, C, 1)
    core_weights = core_own, shifted(plane_weight, C, 1)

    position = jnp.sum(
        jnp.where(
            row_adapter[:, 0][:, None] == jnp.arange(pool, dtype=jnp.int32)[None, :],
            holder_slot[None, :],
            0,
        ),
        axis=1,
    )
    grouped = position.reshape(n_z, -1)
    group_rows = grouped.shape[1]
    earlier = (
        jnp.arange(group_rows, dtype=jnp.int32)[:, None]
        > jnp.arange(group_rows, dtype=jnp.int32)[None, :]
    )
    place = jnp.sum(
        jnp.where(earlier[None] & (grouped[:, :, None] == grouped[:, None, :]), 1, 0), axis=2
    ).astype(jnp.int32)

    paired = line_rows.reshape(n_z // 2, 2, block_rows, -1)
    kept = lax.dynamic_index_in_dim(paired, me_zl, 1, keepdims=False)
    given = lax.dynamic_index_in_dim(paired, 1 - me_zl, 1, keepdims=False)
    taken = shifted(given, ZL, 1)
    blocks = jnp.stack([kept, taken])
    across = [blocks] + [shifted(blocks, X, step) for step in range(1, n_x)]

    def of_line(table):
        blocks = table.reshape(n_z, n_x * n_c, block_rows)
        return lax.dynamic_index_in_dim(blocks, me_x * n_c + me_c, 1, keepdims=False).reshape(-1)

    line_position, line_place = of_line(grouped), of_line(place)
    held_x = (me_x - jnp.arange(n_x, dtype=jnp.int32)) % n_x
    low = []
    for factors, core in ((near, me_c), (far, 1 - me_c)):
        held = (me_y * n_x + held_x) * n_c + core
        product = jnp.einsum("gik,nk->gin", line_rows, factors, preferred_element_type=F32)
        product = product.reshape(n_z * block_rows, n_x, rank)
        low.append(
            jnp.sum(
                jnp.where((line_position[:, None] == held[None])[..., None], product, 0.0), axis=1
            )
        )
    low = low[0] + low[1]
    line_group = jnp.arange(n_z * block_rows, dtype=jnp.int32) // block_rows
    local = line_position - me_y * (n_x * n_c)
    slots = n_x * n_c * n_z * CAP
    slot = jnp.where(
        (local >= 0) & (local < n_x * n_c), (local * n_z + line_group) * CAP + line_place, -1
    )
    half = CAP // 2
    slot_half = (slot // half) % 2
    slot_line = jnp.where(slot >= 0, (slot // CAP) * half + slot % half, -1)
    lines = jnp.arange(slots // 2, dtype=jnp.int32)[:, None]
    placed = jnp.concatenate(
        [
            ((lines == slot_line[None, :]) & (slot_half[None, :] == side)).astype(F32)
            for side in range(2)
        ],
        axis=1,
    )
    none = jnp.zeros_like(low)
    sides = jnp.concatenate(
        [jnp.concatenate([low, none], axis=1), jnp.concatenate([none, low], axis=1)], axis=0
    )
    packed = jnp.dot(placed, sides, precision=HIGHEST, preferred_element_type=F32)
    packed = packed.reshape(n_x * n_c * n_z, half, 2 * rank)
    gathered = lax.all_to_all(packed, (X, C, ZH, ZL), 0, 0, tiled=True)

    pieces = expanded(gathered, expand_pool[0], pool, columns)
    received = lax.all_to_all(pieces, WIDE, 0, 0, tiled=True)
    received = received.reshape(pool * CAP, columns)

    weights = [
        jnp.concatenate([own_weight, core_weights[0]], axis=0),
        jnp.concatenate([plane_weight, core_weights[1]], axis=0),
    ]
    rows = jnp.concatenate(across, axis=2)
    partial = sum(
        jnp.einsum("grk,nk->grn", rows[i], weights[i], preferred_element_type=F32)
        for i in range(2)
    )
    base = sum_at_owner(partial)
    mine = jnp.concatenate([base[:, :columns], shifted(base[:, columns:], C, 1)], axis=0)

    group_position = lax.dynamic_index_in_dim(grouped, me_z, 0, keepdims=False)
    group_place = lax.dynamic_index_in_dim(place, me_z, 0, keepdims=False)
    slot_of_row = group_position * CAP + group_place
    chosen = (
        jnp.arange(pool * CAP, dtype=jnp.int32)[:, None] == slot_of_row[None, :]
    ).astype(BF16)
    update = lax.dot_general(
        received, chosen, (((0,), (0,)), ((), ())), preferred_element_type=F32
    )
    row = jnp.arange(group_rows, dtype=jnp.int32)
    block = row // block_rows
    row_x, row_c = block // n_c, block % n_c
    source = (
        (row_c ^ me_c) * n_x + (me_x - row_x) % n_x
    ) * block_rows + row % block_rows
    spread = (jnp.arange(group_rows, dtype=jnp.int32)[:, None] == source[None, :]).astype(F32)
    base_rows = lax.dot_general(
        mine, spread, (((0,), (0,)), ((), ())), precision=HIGHEST, preferred_element_type=F32
    )
    return (base_rows + ADAPTER_SCALE * update).astype(BF16).T


def solution(mesh):
    finer = Mesh(mesh.devices.reshape(8, 4, 2, 4, 2), (Y, X, C, ZH, ZL))

    return jax.shard_map(
        per_device,
        mesh=finer,
        in_specs=(
            P(WIDE, Z),
            P(Z, WIDE),
            P(WIDE, Z, None),
            P(WIDE, None, None),
            P(),
            P(),
        ),
        out_specs=P(Z, WIDE),
        check_vma=False,
    )
```
